32 devices in a mesh: rep: 2 (over core), shard: 4 (over y, x), expert: 4 (over z).
Axes of the slice: x: 2, y: 2, z: 4, core: 2. Of those that a mesh axis runs over, the one named last changes fastest.
Arguments:
- latent: bfloat16 [8, 128, 2048], P(('rep', 'expert'), None, 'shard'), may hold values from -6 to 6
- noise_draw: bfloat16 [8, 128, 2048], P(('rep', 'expert'), None, 'shard'), may hold values from -6 to 6
- noise_level: float32 [8], P(('rep', 'expert')), may hold values from 0.05 to 0.5
- gen_weight: bfloat16 [2048, 2048], P('shard'), may hold values from -0.125 to 0.125
- norm_gain: float32 [2048], replicated, may hold values from 0.5 to 1.5
- routes: int32 [8, 128, 2], P(('rep', 'expert')), may hold values from 0 to 3, all different within a row; in each aligned block of 128 rows (0 to 127, 128 to 255, ..., all dimensions but the last counted through in order) at most 96 rows name the same one
- route_weight: bfloat16 [8, 128, 2], P(('rep', 'expert')), may hold values from 0.25 to 1
- up_weight: bfloat16 [4, 2048, 4096], P('expert', None, 'shard'), may hold values from -0.125 to 0.125
- down_weight: bfloat16 [4, 2048, 4096], P('expert', None, 'shard'), may hold values from -0.09375 to 0.09375
Outputs:
- denoise_err: bfloat16 [8, 128, 2048], P(('rep', 'expert'), None, 'shard')
- grad_up: float32 [4, 2048, 4096], P('expert', 'rep', 'shard')
- grad_down: float32 [4, 2048, 4096], P('expert', 'rep', 'shard')
The draws below stay inside these ranges and needn't reach their ends.
Inputs may be any that keep to these rules, and one draw needn't show every extreme that they name: `routes`: within one latent no expert is named by more than 96 tokens, and in every draw some expert is named by exactly 96 tokens of some latent; each token names 2 different experts.
All inputs are finite; a program needn't handle non-finite values.
Results may differ from the reference program's by a relative error of at most 0.025.
Values may be sent and summed in bfloat16 or wider, within the bound.
No kernel may reach another device: no remote copies, remote signals or barrier semaphores. Data moves between devices by JAX's collectives and lax.ppermute only.
A program may use at most 64 MiB of HBM per device.

```python
import math
import jax
import jax.numpy as jnp
import numpy as np
from jax import lax

D = 2048
HID = 4096
TOP = 2
EXPERTS = 4
TOK_GRP = 128
CAP = 96
BATCH = 8
N_REP = 2
N_SHARD = 4


def block_levels(key, shape, pieces, least, high):
    def one(dim, parts):
        heights = jax.random.uniform(jax.random.fold_in(jax.random.fold_in(key, 6), dim), (parts,), jnp.float32, least / len(pieces), high / len(pieces))
        return jnp.repeat(jnp.exp(heights), shape[dim] // parts).reshape((-1,) + (1,) * (len(shape) - dim - 1))

    gain = one(*pieces[0])
    for cut in pieces[1:]:
        gain = gain * one(*cut)
    return gain


def routed_block(own_key, own, number, rows, number_of, top, limit, skew):
    sequence = jax.random.permutation(own_key, number_of)
    crowded, common = shares(number_of, rows * top, limit, skew, True), shares(number_of, rows * top, limit, skew, False)
    places = jnp.arange(number_of)

    def named(lengths, turn):
        used = int((lengths > 0).sum())
        fixed = max(1, used // 4)
        passed = fixed + (places - fixed + turn * (used - fixed)) % max(1, number_of - fixed)
        return jnp.zeros((number_of,), jnp.int32).at[sequence[jnp.where(places < fixed, places, passed)]].set(jnp.asarray(lengths, jnp.int32))

    lengths = jnp.where(number % 4 == 0, named(crowded, number // 4), named(common, number - number // 4 - 1))
    mixed = jax.random.permutation(jax.random.fold_in(own, 3), number_of)
    giver, receiver = mixed[0:number_of // 2 * 2:2], mixed[1:number_of // 2 * 2:2]
    room = jnp.minimum(lengths[giver] - 1, limit - lengths[receiver]) // 2
    room = jnp.where((giver == sequence[0]) | (receiver == sequence[0]) | (lengths[receiver] == 0), 0, jnp.maximum(room, 0))
    passed = jax.random.randint(jax.random.fold_in(own, 4), (number_of // 2,), 0, 1 << 20) % (room + 1)
    lengths = lengths.at[giver].add(-passed).at[receiver].add(passed)
    items = jnp.searchsorted(jnp.cumsum(lengths), jnp.arange(rows * top), side="right").astype(jnp.int32)
    table = items.reshape(top, rows).T
    table = table[jax.random.permutation(jax.random.fold_in(own, 1), rows)]
    turn = jax.random.randint(jax.random.fold_in(own, 2), (rows, 1), 0, top)
    return jnp.take_along_axis(table, (jnp.arange(top)[None, :] + turn) % top, axis=1)


def shares(number_of, total, bound, skew, full):
    weights = [(1 << 20) // math.isqrt(grade ** skew) + 1 for grade in range(1, number_of + 1)]
    largest = bound if full else min(bound, max(-(-total // number_of), total * weights[0] // sum(weights)))
    least = 1 if total - largest >= number_of - 1 else 0
    holding, surplus = [largest] + [least] * (number_of - 1), total - largest - least * (number_of - 1)
    while surplus > 0:
        free = [i for i in range(1, number_of) if holding[i] < largest] or [i for i in range(1, number_of) if holding[i] < bound]
        whole, budget = sum([weights[i] for i in free]), surplus
        for i in free:
            addition = min(bound - holding[i], max(1, budget * weights[i] // whole), surplus)
            holding[i] = holding[i] + addition
            surplus = surplus - addition
    return np.array(holding)


def centred(rng, dims, width, limit, split=(), kind=jnp.bfloat16):
    level = block_levels(rng, dims, split, -0.22, 0.18) if split else 1.0
    values = jax.random.normal(rng, dims, jnp.float32) * width * level
    return jnp.minimum(jnp.maximum(values, -limit), limit).astype(kind)


def setup_inputs(seed: int = 0) -> dict:
    seeds = jax.random.split(jax.random.key(seed), 10)
    latent = centred(seeds[0], (BATCH, TOK_GRP, D), 1.0, 6.0, ((0, 8), (2, 4)))
    noise_draw = centred(seeds[1], (BATCH, TOK_GRP, D), 1.0, 6.0, ((0, 8), (2, 4)))
    noise_level = jnp.clip(jnp.exp(math.log(0.5) - 2.3025851 * jax.random.uniform(seeds[2], (BATCH,), jnp.float32) ** block_levels(seeds[2], (BATCH,), ((0, 8),), -0.2, 0.2)), 0.05, 0.5)
    gen_weight = centred(seeds[3], (D, D), D ** -0.5, 0.125, ((0, 4),))
    norm_gain = jnp.clip(1.0 + 0.1 * jax.random.normal(seeds[4], (D,), jnp.float32), 0.5, 1.5)
    routes_keys = jax.random.split(jax.random.fold_in(seeds[5], 1), BATCH * TOK_GRP // TOK_GRP)
    routes_turns = jax.random.permutation(jax.random.fold_in(seeds[5], 3), BATCH * TOK_GRP // TOK_GRP)
    routes = jax.vmap(lambda own, number: routed_block(jax.random.fold_in(seeds[5], 2), own, number, TOK_GRP, EXPERTS, TOP, CAP, 2))(routes_keys, routes_turns).reshape((BATCH, TOK_GRP, TOP))
    route_weight = jnp.clip(0.25 + 0.75 * jax.random.uniform(seeds[6], (BATCH, TOK_GRP, TOP), jnp.float32) ** block_levels(seeds[6], (BATCH, TOK_GRP, TOP), ((0, 8),), -0.2, 0.2), 0.25, 1.0).astype(jnp.bfloat16)
    up_weight = centred(seeds[7], (EXPERTS, D, HID), D ** -0.5, 0.125, ((0, 4), (2, 4)))
    down_weight = centred(seeds[8], (EXPERTS, D, HID), HID ** -0.5, 0.09375, ((0, 4), (2, 4)))
    return {"latent": latent, "noise_draw": noise_draw, "noise_level": noise_level, "gen_weight": gen_weight, "norm_gain": norm_gain, "routes": routes, "route_weight": route_weight, "up_weight": up_weight, "down_weight": down_weight}


epsilon = 1e-06

def normalize(values, gain_vector):
    inverse_rms = lax.rsqrt(lax.optimization_barrier(jnp.mean(values * values, axis=-1, keepdims=True)) + epsilon)
    return values * inverse_rms * gain_vector

def slot_table(routes):
    expert_iota = jnp.arange(EXPERTS, dtype=jnp.int32)
    chosen = (routes[..., None] == expert_iota).astype(jnp.int32)
    per_token = lax.optimization_barrier(jnp.sum(chosen, axis=-2))
    earlier = jnp.cumsum(per_token, axis=-2) - per_token
    return lax.optimization_barrier(jnp.sum(earlier[..., None, :] * chosen, axis=-1)).astype(jnp.int32)

def expert_forward(operands):
    inputs, weight_in, weight_out = operands
    flat_rows = inputs.reshape(-1, D)
    preact = jnp.dot(flat_rows, weight_in, preferred_element_type=jnp.float32)
    hidden = jax.nn.gelu(preact).astype(jnp.bfloat16)
    blocks = hidden.astype(jnp.float32).reshape(-1, N_SHARD, HID // N_SHARD)
    out_blocks = weight_out.astype(jnp.float32).reshape(D, N_SHARD, HID // N_SHARD)
    partial_out = jnp.einsum('msh,dsh->msd', blocks, out_blocks).astype(jnp.bfloat16)
    partial_out = lax.optimization_barrier(partial_out)
    summed = lax.optimization_barrier(jnp.sum(partial_out.astype(jnp.float32), axis=1))
    return summed.reshape(inputs.shape)

def expert_backward(operands):
    inputs, grads_out, weight_in, weight_out = operands
    flat_rows = inputs.reshape(-1, D)
    flat_grads = grads_out.reshape(-1, D)
    preact = jnp.dot(flat_rows, weight_in, preferred_element_type=jnp.float32)
    hidden = jax.nn.gelu(preact).astype(jnp.bfloat16)
    grad_hidden = jnp.dot(flat_grads, weight_out, preferred_element_type=jnp.float32)
    grad_pre = jax.vjp(jax.nn.gelu, preact)[1](grad_hidden)[0].astype(jnp.bfloat16)
    rep_rows = flat_rows.astype(jnp.float32).reshape(N_REP, -1, D)
    rep_grads = flat_grads.astype(jnp.float32).reshape(N_REP, -1, D)
    rep_pre = grad_pre.astype(jnp.float32).reshape(N_REP, -1, HID)
    rep_hidden = hidden.astype(jnp.float32).reshape(N_REP, -1, HID)
    up_terms = jnp.einsum('rmd,rmh->rdh', rep_rows, rep_pre).astype(jnp.bfloat16)
    down_terms = jnp.einsum('rmd,rmh->rdh', rep_grads, rep_hidden).astype(jnp.bfloat16)
    up_terms = lax.optimization_barrier(up_terms)
    down_terms = lax.optimization_barrier(down_terms)
    return (lax.optimization_barrier(jnp.sum(up_terms.astype(jnp.float32), axis=0)), lax.optimization_barrier(jnp.sum(down_terms.astype(jnp.float32), axis=0)))

def reference(latent, noise_draw, noise_level, gen_weight, norm_gain, routes, route_weight, up_weight, down_weight):
    latent_flat = latent.reshape(-1, D)
    projected = jnp.dot(latent_flat, gen_weight, preferred_element_type=jnp.float32).reshape(latent.shape)
    generated = (latent.astype(jnp.float32) + projected).astype(jnp.bfloat16)
    noise_term = noise_level[:, None, None] * noise_draw.astype(jnp.float32)
    normed = normalize(generated.astype(jnp.float32) + noise_term, norm_gain).astype(jnp.bfloat16)
    slot_index = slot_table(routes)
    batch_index = jnp.broadcast_to(jnp.arange(BATCH, dtype=jnp.int32)[:, None, None], routes.shape)
    spread = jnp.broadcast_to(normed[:, :, None, :], routes.shape + (D,))
    dispatched = jnp.zeros((EXPERTS, BATCH, CAP, D), jnp.bfloat16).at[routes, batch_index, slot_index].set(spread)
    outputs = lax.map(expert_forward, (dispatched, up_weight, down_weight))
    picked = outputs[routes, batch_index, slot_index]
    mixture = lax.optimization_barrier(jnp.sum(route_weight.astype(jnp.float32)[..., None] * picked, axis=2))
    denoise_err = (mixture + noise_term).astype(jnp.bfloat16)
    grads_rows = (route_weight.astype(jnp.float32)[..., None] * denoise_err.astype(jnp.float32)[:, :, None, :]).astype(jnp.bfloat16)
    grad_buffer = jnp.zeros((EXPERTS, BATCH, CAP, D), jnp.bfloat16).at[routes, batch_index, slot_index].set(grads_rows)
    grad_up, grad_down = lax.map(expert_backward, (dispatched, grad_buffer, up_weight, down_weight))
    return (denoise_err, grad_up, grad_down)
```

```python
import jax
import jax.numpy as jnp
from jax import lax
from jax.sharding import PartitionSpec as P

epsilon = 1e-06
direct_limit = 4


def contract_rows(left_side, right_side):
    return lax.dot_general(
        left_side, right_side, (((0,), (0,)), ((), ())), preferred_element_type=jnp.float32
    )


def swap(values, axis, step):
    if step == 0:
        return values
    pairs = [(i, i ^ step) for i in range(lax.axis_size(axis))]
    return lax.ppermute(values, axis, pairs)


def reorder(pieces, index):
    bit = 1
    while bit < len(pieces):
        flip = (index & bit) != 0
        pieces = [jnp.where(flip, pieces[i ^ bit], pieces[i]) for i in range(len(pieces))]
        bit *= 2
    return pieces


def gather_columns(values, axis):
    count = lax.axis_size(axis)
    if count > direct_limit:
        return lax.all_gather(values, axis, axis=1, tiled=True)
    pieces = [swap(values, axis, step) for step in range(count)]
    return jnp.concatenate(reorder(pieces, lax.axis_index(axis)), axis=1)


def sum_columns(values, axis):
    count = lax.axis_size(axis)
    width = values.shape[1] // count
    if count > direct_limit:
        blocks = values.astype(jnp.bfloat16).reshape(-1, count, width)
        blocks = lax.all_to_all(blocks, axis, split_axis=1, concat_axis=1, tiled=True)
        return jnp.sum(blocks.astype(jnp.float32), axis=1)
    blocks = [values[:, i * width : (i + 1) * width] for i in range(count)]
    blocks = reorder(blocks, lax.axis_index(axis))
    total = blocks[0].astype(jnp.float32)
    for step in range(1, count):
        total += swap(blocks[step].astype(jnp.bfloat16), axis, step).astype(jnp.float32)
    return total


def per_device(
    latent,
    noise_draw,
    noise_level,
    gen_weight,
    norm_gain,
    routes,
    route_weight,
    up_weight,
    down_weight,
):
    own_latent = latent[0]
    weight_in = up_weight[0]
    weight_out = down_weight[0]
    routes = routes[0]
    sequence, top_count = routes.shape
    owners = lax.axis_size("expert")
    own_experts = up_weight.shape[0]
    experts = own_experts * owners
    capacity = 3 * top_count * sequence // (2 * experts)
    here = lax.axis_index("expert")
    half = own_latent.shape[1] * lax.axis_size("shard") // lax.axis_size("rep")
    rep = lax.axis_index("rep")

    partial_sums = jnp.dot(own_latent, gen_weight, preferred_element_type=jnp.float32)
    projected = sum_columns(partial_sums, "shard")
    generated = (own_latent.astype(jnp.float32) + projected).astype(jnp.bfloat16)
    noise = noise_level[0] * noise_draw[0].astype(jnp.float32)
    noised = (generated.astype(jnp.float32) + noise).astype(jnp.bfloat16)

    expert_iota = jnp.arange(experts, dtype=jnp.int32)
    chosen = (routes[:, :, None] == expert_iota).astype(jnp.int32)
    per_token = jnp.sum(chosen, axis=1)
    earlier = jnp.cumsum(per_token, axis=0) - per_token
    slot_index = jnp.sum(earlier[:, None, :] * chosen, axis=-1)
    target = routes * capacity + slot_index
    weights = route_weight[0].astype(jnp.float32)

    direct = owners <= direct_limit
    steps = range(owners) if direct else range(1)
    rows = capacity * (1 if direct else owners)

    def across(values, step):
        if direct:
            return swap(values, "expert", step)
        blocks = values.reshape(owners, capacity, values.shape[1])
        blocks = lax.all_to_all(blocks, "expert", split_axis=0, concat_axis=0, tiled=True)
        return blocks.reshape(values.shape)

    placements, combines = [], []
    for step in steps:
        first = (here ^ step) * capacity if direct else 0
        matches = target[:, :, None] == first + jnp.arange(rows, dtype=jnp.int32)
        placements.append(jnp.any(matches, axis=1).astype(jnp.bfloat16))
        combines.append(
            jnp.sum(jnp.where(matches, weights[:, :, None], 0.0), axis=1).astype(jnp.bfloat16)
        )

    normed_parts, preact_parts, hidden_parts = [], [], []
    mixture = noise
    for step in steps:
        sent = contract_rows(placements[step], noised).astype(jnp.bfloat16)
        full = gather_columns(across(sent, step), "shard").astype(jnp.float32)
        inverse_rms = lax.rsqrt(jnp.mean(full * full, axis=-1, keepdims=True) + epsilon)
        normed = (full * inverse_rms * norm_gain).astype(jnp.bfloat16)
        preact = jnp.dot(normed, weight_in, preferred_element_type=jnp.float32)
        hidden = jax.nn.gelu(preact).astype(jnp.bfloat16)
        partial_out = lax.dot_general(
            hidden, weight_out, (((1,), (1,)), ((), ())), preferred_element_type=jnp.float32
        ).astype(jnp.bfloat16)
        summed = sum_columns(partial_out, "shard").astype(jnp.bfloat16)
        returned = across(summed, step)
        mixture += jnp.dot(combines[step], returned, preferred_element_type=jnp.float32)
        normed_parts.append(normed)
        preact_parts.append(preact)
        hidden_parts.append(hidden)
    own_err = mixture.astype(jnp.bfloat16)

    grad_parts, pre_parts = [], []
    for step in steps:
        sent = contract_rows(combines[step], own_err).astype(jnp.bfloat16)
        grads = gather_columns(across(sent, step), "shard")
        grad_hidden = jnp.dot(grads, weight_out, preferred_element_type=jnp.float32)
        grad_pre = jax.vjp(jax.nn.gelu, preact_parts[step])[1](grad_hidden)[0]
        grad_parts.append(grads)
        pre_parts.append(grad_pre.astype(jnp.bfloat16))

    reps = lax.axis_size("rep")

    def weight_gradient(wide_parts, narrow_parts):
        lefts, rights = [], []
        for wide, narrow in zip(wide_parts, narrow_parts):
            blocks = reorder([wide[:, i * half : (i + 1) * half] for i in range(reps)], rep)
            for step in range(reps):
                lefts.append(swap(blocks[step], "rep", step))
                rights.append(swap(narrow, "rep", step))
        return contract_rows(jnp.concatenate(lefts, axis=0), jnp.concatenate(rights, axis=0))

    grad_down = weight_gradient(grad_parts, hidden_parts)
    grad_up = weight_gradient(normed_parts, pre_parts)
    return (own_err[None], grad_up[None], grad_down[None])


def solution(mesh):
    in_specs = (
        P(("rep", "expert"), None, "shard"),
        P(("rep", "expert"), None, "shard"),
        P(("rep", "expert")),
        P("shard", None),
        P(),
        P(("rep", "expert"), None, None),
        P(("rep", "expert"), None, None),
        P("expert", None, "shard"),
        P("expert", None, "shard"),
    )
    out_specs = (
        P(("rep", "expert"), None, "shard"),
        P("expert", "rep", "shard"),
        P("expert", "rep", "shard"),
    )
    return jax.shard_map(
        per_device, mesh=mesh, in_specs=in_specs, out_specs=out_specs, check_vma=False
    )
```
